32 devices in a mesh: seg: 4 (over y, core), ep: 8 (over z, x).
Axes of the slice: x: 2, y: 2, z: 4, core: 2. Of those that a mesh axis runs over, the one named last changes fastest.
Arguments:
- queries: bfloat16 [2048, 2048], P(('seg', 'ep')), may hold values from -6 to 6
- keys: bfloat16 [2048, 2048], P(('seg', 'ep')), may hold values from -1.25 to 1.25
- values: bfloat16 [2048, 2048], P(('seg', 'ep')), may hold values from -54 to 54
- log_decay: float32 [2048, 16], P('seg', 'ep'), may hold values from -1 to 0
- out_gain: float32 [2048], replicated, may hold values from 0.1 to 1.9
- out_proj: bfloat16 [2048, 6144], P('ep', 'seg'), may hold values from -0.125 to 0.125
- experts: int32 [256, 2], P(('seg', 'ep')), may hold values from 0 to 3, all different within a row; in each aligned block of 8 rows (0 to 7, 8 to 15, ...) at most 8 rows name the same one
- gates: float32 [256, 2], P(('seg', 'ep')), may hold values from 0.2 to 1
- up_weight: bfloat16 [8, 6144, 2304], P('ep', None, 'seg'), may hold values from -0.078125 to 0.078125
- down_weight: bfloat16 [8, 2304, 6144], P('ep', 'seg'), may hold values from -0.09375 to 0.09375
Outputs:
- attn_out: bfloat16 [2048, 2048], P(('seg', 'ep'))
- moe_out: bfloat16 [256, 6144], P(('seg', 'ep'))
The draws below stay inside these ranges and needn't reach their ends.
Inputs may be any that keep to these rules, and one draw needn't show every extreme that they name: Each row names two different experts. The 8 rows of one device name any one expert at most 8 times, and in some devices one expert exactly 8 times.
All inputs are finite; a program needn't handle non-finite values.
Results may differ from the reference program's by a relative error of at most 0.025.
Values may be sent and summed in bfloat16 or wider, within the bound.
A program may use at most 128 MiB of HBM per device.

```python
import math
import jax
import jax.numpy as jnp
import numpy as np
from jax import lax

D = 6144
HEAD_DIM = 128
EXPERT_FF = 4608
TOK_DEV = 64
MOE_TOK = 8
HEAD_COUNT = 16
EXPERTS = 4
FF_DEV = 576
CAP = 8
SEG_LEN = 512
TOKEN_COUNT = 2048
MOE_TOKENS = 256
N_SEG = 4
DEVICES = 32


def draw_values(key, part):
    key_sequence = jax.random.split(jax.random.fold_in(key, 11), 3)
    columns = HEAD_COUNT * HEAD_DIM
    column_scale = jnp.exp(jax.random.uniform(key_sequence[0], (1, columns), jnp.float32, math.log(0.3), math.log(3.0)))
    row_scale = jnp.exp(jax.random.uniform(key_sequence[1], (TOKEN_COUNT, 1), jnp.float32, math.log(0.3), math.log(3.0)))
    base = jnp.clip(jax.random.normal(key_sequence[2], (TOKEN_COUNT, columns), jnp.float32), -6.0, 6.0)
    return (base * column_scale * row_scale).astype(jnp.bfloat16)


def draw_log_decay(key, part):
    key_sequence = jax.random.split(jax.random.fold_in(key, 23), 6)
    fast_share = 0.5
    fast_heads = jax.random.uniform(key_sequence[0], (HEAD_COUNT,), jnp.float32) < fast_share
    fast_rate = jnp.exp(jax.random.uniform(key_sequence[1], (HEAD_COUNT,), jnp.float32, math.log(1.0 / 50.0), math.log(1.0 / 30.0)))
    slow_rate = 0.25 / TOKEN_COUNT
    baseline_rate = jnp.where(fast_heads, fast_rate, slow_rate)
    block_count = TOKEN_COUNT // TOK_DEV
    block_multiplier = jnp.exp(jax.random.uniform(key_sequence[2], (block_count, HEAD_COUNT), jnp.float32, math.log(0.5), math.log(2.0)))
    block_multiplier = jnp.repeat(block_multiplier, TOK_DEV, axis=0)
    jaggedness = jax.random.uniform(key_sequence[3], (TOKEN_COUNT, HEAD_COUNT), jnp.float32, 0.5, 1.5)
    spike_locations = jax.random.randint(key_sequence[4], (2, HEAD_COUNT), 0, TOKEN_COUNT)
    token_positions = jnp.arange(TOKEN_COUNT, dtype=jnp.int32)[:, None]
    spike_mask = (token_positions == spike_locations[0][None, :]) | (token_positions == spike_locations[1][None, :])
    spike_magnitude = jax.random.uniform(key_sequence[5], (TOKEN_COUNT, HEAD_COUNT), jnp.float32, 0.22, 0.69)
    decay_rate = baseline_rate[None, :] * block_multiplier * jaggedness + jnp.where(spike_mask, spike_magnitude, 0.0)
    return (-decay_rate).astype(jnp.float32)


def block_scale(key, extent, cuts, smallest, high):
    def one(dim, shards_of):
        draws = jax.random.uniform(jax.random.fold_in(jax.random.fold_in(key, 6), dim), (shards_of,), jnp.float32, smallest / len(cuts), high / len(cuts))
        return jnp.repeat(jnp.exp(draws), extent[dim] // shards_of).reshape((-1,) + (1,) * (len(extent) - dim - 1))

    factor_of = one(*cuts[0])
    for cut in cuts[1:]:
        factor_of = factor_of * one(*cut)
    return factor_of


def deal_out(stream_key, own, number, rows, number_of, top, bound, lean):
    sequence = jax.random.permutation(stream_key, number_of)
    crowded, usual = portions_of(number_of, rows * top, bound, lean, True), portions_of(number_of, rows * top, bound, lean, False)
    places = jnp.arange(number_of)

    def named(lengths, rotation):
        used = int((lengths > 0).sum())
        fixed = max(1, used // 4)
        moved = fixed + (places - fixed + rotation * (used - fixed)) % max(1, number_of - fixed)
        return jnp.zeros((number_of,), jnp.int32).at[sequence[jnp.where(places < fixed, places, moved)]].set(jnp.asarray(lengths, jnp.int32))

    lengths = jnp.where(number % 4 == 0, named(crowded, number // 4), named(usual, number - number // 4 - 1))
    mixed = jax.random.permutation(jax.random.fold_in(own, 3), number_of)
    giver, sink = mixed[0:number_of // 2 * 2:2], mixed[1:number_of // 2 * 2:2]
    margin = jnp.minimum(lengths[giver] - 1, bound - lengths[sink]) // 2
    margin = jnp.where((giver == sequence[0]) | (sink == sequence[0]) | (lengths[sink] == 0), 0, jnp.maximum(margin, 0))
    moved = jax.random.randint(jax.random.fold_in(own, 4), (number_of // 2,), 0, 1 << 20) % (margin + 1)
    lengths = lengths.at[giver].add(-moved).at[sink].add(moved)
    members = jnp.searchsorted(jnp.cumsum(lengths), jnp.arange(rows * top), side="right").astype(jnp.int32)
    table = members.reshape(top, rows).T
    table = table[jax.random.permutation(jax.random.fold_in(own, 1), rows)]
    rotation = jax.random.randint(jax.random.fold_in(own, 2), (rows, 1), 0, top)
    return jnp.take_along_axis(table, (jnp.arange(top)[None, :] + rotation) % top, axis=1)


def portions_of(count, total, limit, slope, full):
    loads = [(1 << 20) // math.isqrt(rank ** slope) + 1 for rank in range(1, count + 1)]
    largest = limit if full else min(limit, max(-(-total // count), total * loads[0] // sum(loads)))
    least = 1 if total - largest >= count - 1 else 0
    counts, rest = [largest] + [least] * (count - 1), total - largest - least * (count - 1)
    while rest > 0:
        free = [i for i in range(1, count) if counts[i] < largest] or [i for i in range(1, count) if counts[i] < limit]
        pool, budget = sum([loads[i] for i in free]), rest
        for i in free:
            addition = min(limit - counts[i], max(1, budget * loads[i] // pool), rest)
            counts[i] = counts[i] + addition
            rest = rest - addition
    return np.array(counts)


def normal_values(own_key, dims, deviation, most, cuts=(), kind=jnp.bfloat16):
    values = jax.random.normal(own_key, dims, jnp.float32) * deviation
    if len(cuts) > 0:
        values = block_scale(own_key, dims, cuts, -0.22, 0.18) * values
    return jnp.clip(values, min=-most, max=most).astype(kind)


def setup_inputs(seed: int = 0) -> dict:
    arg_keys = jax.random.split(jax.random.key(seed), 11)
    queries = normal_values(arg_keys[0], (TOKEN_COUNT, HEAD_COUNT * HEAD_DIM), 1.0, 6.0, ((0, 32),))
    keys = normal_values(arg_keys[1], (TOKEN_COUNT, HEAD_COUNT * HEAD_DIM), (HEAD_DIM ** -0.5), 1.25, ((0, 32),))
    values = draw_values(jax.random.fold_in(arg_keys[10], 71), 0)
    log_decay = draw_log_decay(jax.random.fold_in(arg_keys[10], 71), 0)
    out_gain = jnp.clip(1.0 + 0.18 * jax.random.normal(arg_keys[4], (HEAD_COUNT * HEAD_DIM,), jnp.float32), 0.1, 1.9)
    out_proj = normal_values(arg_keys[5], (HEAD_COUNT * HEAD_DIM, D), (HEAD_COUNT * HEAD_DIM) ** -0.5, 0.125, ((0, 8), (1, 4)))
    experts_keys = jax.random.split(jax.random.fold_in(arg_keys[6], 1), MOE_TOKENS // MOE_TOK)
    experts_turns = jax.random.permutation(jax.random.fold_in(arg_keys[6], 3), MOE_TOKENS // MOE_TOK)
    experts = jax.vmap(lambda own, number: deal_out(jax.random.fold_in(arg_keys[6], 2), own, number, MOE_TOK, EXPERTS, 2, CAP, 2))(experts_keys, experts_turns).reshape((MOE_TOKENS, 2))
    gates = jnp.clip(0.2 + 0.8 * jax.random.uniform(arg_keys[7], (MOE_TOKENS, 2), jnp.float32) ** block_scale(arg_keys[7], (MOE_TOKENS, 2), ((0, 32),), -0.2, 0.2), 0.2, 1.0)
    up_weight = normal_values(arg_keys[8], (2 * EXPERTS, D, EXPERT_FF // 2), D ** -0.5, 0.078125, ((0, 8), (2, 4)))
    down_weight = normal_values(arg_keys[9], (2 * EXPERTS, EXPERT_FF // 2, D), EXPERT_FF ** -0.5, 0.09375, ((0, 8), (1, 4)))
    return {"queries": queries, "keys": keys, "values": values, "log_decay": log_decay, "out_gain": out_gain, "out_proj": out_proj, "experts": experts, "gates": gates, "up_weight": up_weight, "down_weight": down_weight}


def reference(queries, keys, values, log_decay, out_gain, out_proj, experts, gates, up_weight, down_weight):
    highest = lax.Precision.HIGHEST
    grid = (N_SEG, SEG_LEN, HEAD_COUNT, HEAD_DIM)
    query_groups = queries.reshape(grid).astype(jnp.float32)
    key_groups = keys.reshape(grid).astype(jnp.float32)
    value_groups = values.reshape(grid).astype(jnp.float32)
    decay_groups = log_decay.reshape(N_SEG, SEG_LEN, HEAD_COUNT)
    causal_mask = jnp.arange(SEG_LEN)[:, None] >= jnp.arange(SEG_LEN)[None, :]

    def head_inside(inputs):
        query_head, key_head, value_head, cum_head = inputs
        log_gap = cum_head[:, None] - cum_head[None, :]
        weight = jnp.where(causal_mask, jnp.exp(jnp.where(causal_mask, log_gap, 0.0)), 0.0)
        scores = jnp.dot(query_head, key_head.T, precision=highest)
        mixing = lax.optimization_barrier((scores * weight).astype(jnp.bfloat16)).astype(jnp.float32)
        return jnp.dot(mixing, value_head, precision=highest)

    def group_step(state, inputs):
        query_block, key_block, value_block, decay_block = inputs
        cumulative = jnp.cumsum(decay_block, axis=0)
        inside = lax.map(head_inside, (query_block.transpose(1, 0, 2), key_block.transpose(1, 0, 2), value_block.transpose(1, 0, 2), cumulative.T)).transpose(1, 0, 2)
        outside = jnp.exp(cumulative)[:, :, None] * jnp.einsum('thd,hde->the', query_block, state, precision=highest)
        mixture = (inside + outside).astype(jnp.bfloat16)
        ending = cumulative[-1]
        to_end = jnp.exp(ending[None, :] - cumulative)
        local_state = jnp.einsum('sh,shd,she->hde', to_end, key_block, value_block, precision=highest)
        new_state = jnp.exp(ending)[:, None, None] * state + local_state
        return (new_state, mixture)
    start_state = jnp.zeros((HEAD_COUNT, HEAD_DIM, HEAD_DIM), jnp.float32)
    final_state, mixtures = lax.scan(group_step, start_state, (query_groups, key_groups, value_groups, decay_groups))
    heads_mix = mixtures.reshape(TOKEN_COUNT, HEAD_COUNT * HEAD_DIM).astype(jnp.float32)
    inv_rms = lax.rsqrt(lax.optimization_barrier(jnp.mean(heads_mix * heads_mix, axis=1, keepdims=True)) + 1e-06)
    attn_out = (heads_mix * inv_rms * out_gain[None, :]).astype(jnp.bfloat16)
    selected = attn_out.reshape(MOE_TOKENS, TOKEN_COUNT // MOE_TOKENS, HEAD_COUNT * HEAD_DIM)[:, 0]
    moe_in = jnp.dot(selected, out_proj, preferred_element_type=jnp.float32).astype(jnp.bfloat16)
    flattened = experts.reshape(DEVICES, 2 * MOE_TOK)
    onehot = (flattened[:, :, None] == jnp.arange(EXPERTS, dtype=jnp.int32)[None, None, :]).astype(jnp.int32)
    earlier = jnp.cumsum(onehot, axis=1) - onehot
    position = lax.optimization_barrier(jnp.sum(earlier * onehot, axis=2)).astype(jnp.int32)
    slot_of = position.reshape(DEVICES, MOE_TOK, 2)
    expert_of = experts.reshape(DEVICES, MOE_TOK, 2)
    rows_by_device = moe_in.reshape(DEVICES, MOE_TOK, D).astype(jnp.float32)
    capacity_ids = jnp.arange(CAP, dtype=jnp.int32)

    def per_expert(expert):
        matches = (expert_of == expert)[:, :, :, None] & (slot_of[:, :, :, None] == capacity_ids[None, None, None, :])
        chosen = jnp.any(matches, axis=2).astype(jnp.float32)
        row_data = jnp.einsum('dtc,dtk->dck', chosen, rows_by_device, precision=highest)
        row_data = row_data.astype(jnp.bfloat16).reshape(DEVICES * CAP, D)
        running = jnp.zeros((DEVICES * CAP, D), jnp.float32)
        for half_index in range(2):
            row_index = (2 * expert + half_index).astype(jnp.int32)
            up_half = lax.dynamic_index_in_dim(up_weight, row_index, 0, keepdims=False)
            down_half = lax.dynamic_index_in_dim(down_weight, row_index, 0, keepdims=False)
            hidden = jax.nn.silu(jnp.dot(row_data, up_half, preferred_element_type=jnp.float32)).astype(jnp.bfloat16)
            hidden_pieces = hidden.reshape(DEVICES * CAP, N_SEG, FF_DEV).astype(jnp.float32)
            down_pieces = down_half.reshape(N_SEG, FF_DEV, D).astype(jnp.float32)
            slice_terms = jnp.einsum('rgk,gkd->grd', hidden_pieces, down_pieces, precision=highest)
            rounded = lax.optimization_barrier(slice_terms.astype(jnp.bfloat16)).astype(jnp.float32)
            running = running + lax.optimization_barrier(jnp.sum(rounded, axis=0))
        return running
    results = lax.map(per_expert, jnp.arange(EXPERTS, dtype=jnp.int32))
    device_index = jnp.arange(DEVICES, dtype=jnp.int32)[:, None, None]
    flat_index = (expert_of * (DEVICES * CAP) + device_index * CAP + slot_of).astype(jnp.int32)
    picked = results.reshape(EXPERTS * DEVICES * CAP, D)[flat_index.reshape(-1)].reshape(DEVICES, MOE_TOK, 2, D)
    weighted = lax.optimization_barrier(jnp.sum(picked * gates.reshape(DEVICES, MOE_TOK, 2, 1), axis=2))
    moe_out = weighted.astype(jnp.bfloat16).reshape(MOE_TOKENS, D)
    return (attn_out, moe_out)
```

```python
import functools
import math

import jax
import jax.numpy as jnp
from jax import lax
from jax.experimental import pallas as pl
from jax.experimental.pallas import tpu as pltpu
from jax.sharding import PartitionSpec as P

epsilon = 1e-06
MESH = pl.DeviceIdType.MESH
VM = pltpu.VMEM


def prefix(x, axis, join, neutral):
    place = lax.axis_index(axis)
    gathered = jax.tree.map(
        lambda a, kind: lax.all_gather(a.astype(kind), axis), x, (jnp.bfloat16, jnp.bfloat16)
    )
    state = jax.tree.map(lambda a, e: jnp.zeros_like(a) + jnp.asarray(e, a.dtype), x, neutral)

    def one(turn, state):
        return join(
            state,
            jax.tree.map(
                lambda a, own: lax.dynamic_index_in_dim(a, turn, 0, False).astype(own.dtype),
                gathered,
                x,
            ),
        )

    return lax.fori_loop(0, place, one, state)


def chain_combine(first_part, second_part):
    return (
        first_part[0] * second_part[0],
        second_part[0][:, None, None] * first_part[1] + second_part[1],
    )


def route_tables(experts, gates, expert_count, capacity):
    token_count = experts.shape[0]
    flattened = experts.reshape(-1)
    onehot = (flattened[:, None] == jnp.arange(expert_count, dtype=jnp.int32)[None, :]).astype(
        jnp.int32
    )
    earlier = jnp.cumsum(onehot, axis=0) - onehot
    position = jnp.sum(earlier * onehot, axis=1)
    slot_index = (flattened * capacity + position).reshape(token_count, 2)
    columns = jnp.arange(expert_count * capacity, dtype=jnp.int32)
    matches = slot_index[:, :, None] == columns[None, None, :]
    dispatch = jnp.any(matches, axis=1).T.astype(jnp.bfloat16)
    combine = jnp.sum(jnp.where(matches, gates[:, :, None], 0.0), axis=1)
    return (dispatch, combine)


def expert_output(row_data, up_piece, down_piece):
    hidden = jax.nn.silu(jnp.dot(row_data, up_piece, preferred_element_type=jnp.float32)).astype(
        jnp.bfloat16
    )
    return jnp.dot(hidden, down_piece, preferred_element_type=jnp.float32)


def on_device_routed(
    queries, keys, values, log_decay, out_gain, out_proj, experts, gates, up_weight, down_weight
):
    highest = lax.Precision.HIGHEST
    ep_count = lax.axis_size("ep")
    heads_local = log_decay.shape[1]
    head_dim = queries.shape[1] // (heads_local * ep_count)
    query_heads, key_heads, value_heads = (
        lax.all_to_all(queries, "ep", split_axis=1, concat_axis=0, tiled=True),
        lax.all_to_all(keys, "ep", split_axis=1, concat_axis=0, tiled=True),
        lax.all_to_all(values, "ep", split_axis=1, concat_axis=0, tiled=True),
    )
    seg_length = query_heads.shape[0]
    query_heads = query_heads.reshape(seg_length, heads_local, head_dim)
    key_heads = key_heads.reshape(seg_length, heads_local, head_dim)
    value_heads = value_heads.reshape(seg_length, heads_local, head_dim)
    cumulative = jnp.cumsum(log_decay, axis=0)
    across = cumulative.T
    block_size = math.gcd(seg_length, 512)
    starts = jnp.arange(seg_length // block_size, dtype=jnp.int32) * block_size
    token_positions = jnp.arange(seg_length, dtype=jnp.int32)

    def block_mix(start):
        query_block = lax.dynamic_slice_in_dim(query_heads, start, block_size, 0)
        cum_block = lax.dynamic_slice_in_dim(across, start, block_size, 1)
        row_ids = start + jnp.arange(block_size, dtype=jnp.int32)
        causal = (row_ids[:, None] >= token_positions[None, :])[None]
        log_gap = cum_block[:, :, None] - across[:, None, :]
        weight = jnp.where(causal, jnp.exp(jnp.where(causal, log_gap, 0.0)), 0.0)
        scores = jnp.einsum(
            "thd,shd->hts", query_block, key_heads, preferred_element_type=jnp.float32
        )
        mixing = (scores * weight).astype(jnp.bfloat16)
        return jnp.einsum("hts,she->the", mixing, value_heads, preferred_element_type=jnp.float32)

    inside = lax.map(block_mix, starts).reshape(seg_length, heads_local, head_dim)
    ending = cumulative[-1]
    to_end = jnp.exp(ending[None, :] - cumulative)
    key_float = key_heads.astype(jnp.float32)
    value_float = value_heads.astype(jnp.float32)
    local_state = jnp.einsum("sh,shd,she->hde", to_end, key_float, value_float, precision=highest)
    identity = (jnp.ones_like(ending), jnp.zeros_like(local_state))
    carried = prefix((jnp.exp(ending), local_state), "seg", chain_combine, identity)[1]
    outside = jnp.exp(cumulative)[:, :, None] * jnp.einsum(
        "thd,hde->the", query_heads.astype(jnp.float32), carried, precision=highest
    )
    mixture = (inside + outside).astype(jnp.bfloat16).reshape(seg_length, heads_local * head_dim)
    token_mix = lax.all_to_all(mixture, "ep", split_axis=0, concat_axis=1, tiled=True)
    as_float = token_mix.astype(jnp.float32)
    inv_rms = lax.rsqrt(jnp.mean(as_float * as_float, axis=1, keepdims=True) + epsilon)
    attn_out = (as_float * inv_rms * out_gain[None, :]).astype(jnp.bfloat16)
    row_stride = 8
    own_width = heads_local * head_dim
    feature_count = own_width * ep_count
    picked_float = mixture.reshape(seg_length // row_stride, row_stride, own_width)[:, 0].astype(
        jnp.float32
    )
    square_sums = lax.psum(jnp.sum(picked_float * picked_float, axis=1), "ep")
    picked_rms = lax.rsqrt(square_sums[:, None] / feature_count + epsilon)
    gain_slice = lax.dynamic_slice_in_dim(out_gain, lax.axis_index("ep") * own_width, own_width, 0)
    normed_rows = (picked_float * picked_rms * gain_slice[None, :]).astype(jnp.bfloat16)
    proj_terms = jnp.dot(
        normed_rows,
        lax.all_gather(out_proj, "seg", axis=1, tiled=True),
        preferred_element_type=jnp.float32,
    )
    moe_in = lax.psum_scatter(
        proj_terms.astype(jnp.bfloat16), "ep", scatter_dimension=0, tiled=True
    )
    expert_count = ep_count // 2
    token_count, model_width = moe_in.shape
    capacity = max(2, 4 * token_count // expert_count)
    dispatch, combine = route_tables(experts, gates, expert_count, capacity)
    up_piece = up_weight[0]
    down_piece = down_weight[0]
    slot_rows = jnp.dot(dispatch, moe_in, preferred_element_type=jnp.float32).astype(jnp.bfloat16)
    outgoing = jnp.repeat(slot_rows.reshape(expert_count, capacity, model_width), 2, axis=0)
    arrived = lax.all_to_all(outgoing, "ep", split_axis=0, concat_axis=0, tiled=True).reshape(
        ep_count * capacity, model_width
    )
    gathered = lax.all_gather(arrived, "seg", axis=0, tiled=True)
    owned_sums = lax.psum_scatter(
        expert_output(gathered, up_piece, down_piece).astype(jnp.bfloat16),
        "seg",
        scatter_dimension=0,
        tiled=True,
    ).astype(jnp.float32)
    returned_back = lax.all_to_all(
        owned_sums.reshape(ep_count, capacity, model_width).astype(jnp.bfloat16),
        "ep",
        split_axis=0,
        concat_axis=0,
        tiled=True,
    ).astype(jnp.float32)
    paired = returned_back.reshape(expert_count, 2, capacity, model_width)
    halves = (paired[:, 0] + paired[:, 1]).reshape(expert_count * capacity, model_width)
    summed = jnp.dot(combine, halves, precision=highest)
    moe_out = summed.astype(jnp.bfloat16)
    return (attn_out, moe_out)


def remote(src, dst, send, recv, **target):
    return pltpu.make_async_remote_copy(
        src_ref=src, dst_ref=dst, send_sem=send, recv_sem=recv,
        device_id=target, device_id_type=MESH,
    )


def greet(seg_count, ep_count):
    seg, ep = lax.axis_index("seg"), lax.axis_index("ep")
    barrier = pltpu.get_barrier_semaphore()
    for j in range(1, ep_count):
        pl.semaphore_signal(
            barrier, inc=1, device_id={"ep": lax.rem(ep + j, ep_count)}, device_id_type=MESH
        )
    for k in range(1, seg_count):
        pl.semaphore_signal(
            barrier, inc=1, device_id={"seg": lax.rem(seg + k, seg_count)}, device_id_type=MESH
        )
    pl.semaphore_wait(barrier, ep_count + seg_count - 2)
    return seg, ep


def mix_kernel(
    seg_count, ep_count, heads, dim,
    q_ref, k_ref, v_ref, cum_ref, across_ref, gate_ref,
    mix_ref, picked_ref, table_ref,
    qb, kb, vb, states, ends,
    in_send, in_recv, gate_send, gate_recv, st_send, st_recv, end_send, end_recv, row_send, row_recv,
):
    seg, ep = greet(seg_count, ep_count)
    width = heads * dim
    triples = ((q_ref, qb), (k_ref, kb), (v_ref, vb))
    table_ref[seg, ep] = gate_ref[...]
    sends, gates = [], []
    for j in range(1, ep_count):
        other = lax.rem(ep + j, ep_count)
        columns = pl.ds(pl.multiple_of(other * width, width), width)
        for i, (ref, buf) in enumerate(triples):
            copy = remote(
                ref.at[:, columns], buf.at[ep], in_send.at[i, j], in_recv.at[i, j], ep=other
            )
            copy.start()
            sends.append(copy)
        copy = remote(
            gate_ref, table_ref.at[seg, ep], gate_send.at[j], gate_recv.at[j], ep=other
        )
        copy.start()
        gates.append(copy)
    own = pl.ds(pl.multiple_of(ep * width, width), width)
    for ref, buf in triples:
        buf[ep] = ref[:, own]
    for copy in sends:
        copy.wait()
    length = q_ref.shape[0] * ep_count
    queries, keys, values = (
        jnp.concatenate([b[p] for p in range(ep_count)], axis=0) for b in (qb, kb, vb)
    )
    cum, across = cum_ref[...], across_ref[...]
    ending = cum[length - 1 : length, :]
    unit = (
        lax.broadcasted_iota(jnp.int32, (dim, dim), 0)
        == lax.broadcasted_iota(jnp.int32, (dim, dim), 1)
    ).astype(jnp.float32).astype(jnp.bfloat16)
    for h in range(heads):
        cols = slice(h * dim, (h + 1) * dim)
        to_end = jnp.exp(ending[:, h : h + 1] - across[h : h + 1, :])
        turned = lax.dot_general(
            unit, keys[:, cols], (((1,), (1,)), ((), ())), preferred_element_type=jnp.float32
        )
        states[seg, h] = jnp.dot(
            (turned * to_end).astype(jnp.bfloat16), values[:, cols],
            preferred_element_type=jnp.float32,
        ).astype(jnp.bfloat16)
        ends[seg, h : h + 1] = jnp.broadcast_to(ending[:, h : h + 1], (1, dim))
    for copy in gates:
        copy.wait()
    moved = []
    for k in range(1, seg_count):
        other = lax.rem(seg + k, seg_count)
        for buf, send, recv in (
            (states, st_send, st_recv), (ends, end_send, end_recv), (table_ref, row_send, row_recv)
        ):
            copy = remote(buf.at[seg], buf.at[seg], send.at[k], recv.at[k], seg=other)
            copy.start()
            moved.append(copy)
    rows = lax.broadcasted_iota(jnp.int32, (length, length), 0)
    columns = lax.broadcasted_iota(jnp.int32, (length, length), 1)
    causal = rows >= columns
    inside = []
    for h in range(heads):
        cols = slice(h * dim, (h + 1) * dim)
        gap = cum[:, h : h + 1] - across[h : h + 1, :]
        weight = jnp.where(causal, jnp.exp(jnp.where(causal, gap, 0.0)), 0.0)
        scores = lax.dot_general(
            queries[:, cols], keys[:, cols], (((1,), (1,)), ((), ())),
            preferred_element_type=jnp.float32,
        )
        inside.append(
            jnp.dot(
                (scores * weight).astype(jnp.bfloat16), values[:, cols],
                preferred_element_type=jnp.float32,
            )
        )
    for copy in moved:
        copy.wait()
    outs = []
    for h in range(heads):
        cols = slice(h * dim, (h + 1) * dim)
        carried = jnp.zeros((dim, dim), jnp.float32)
        for c in range(seg_count):
            joined = jnp.exp(ends[c, h : h + 1]) * carried + states[c, h].astype(jnp.float32)
            carried = jnp.where(c < seg, joined, carried)
        outside = jnp.exp(cum[:, h : h + 1]) * jnp.dot(
            queries[:, cols], carried.astype(jnp.bfloat16), preferred_element_type=jnp.float32
        )
        outs.append((inside[h] + outside).astype(jnp.bfloat16))
    mixture = jnp.concatenate(outs, axis=1)
    mix_ref[...] = mixture.reshape(mix_ref.shape)
    count = picked_ref.shape[0]
    stride = length // count
    pick = (
        lax.broadcasted_iota(jnp.int32, (count, length), 1)
        == stride * lax.broadcasted_iota(jnp.int32, (count, length), 0)
    )
    picked_ref[...] = jnp.dot(
        pick.astype(jnp.float32).astype(jnp.bfloat16), mixture, preferred_element_type=jnp.float32
    ).astype(jnp.bfloat16)


def expert_kernel(
    seg_count, ep_count, tile,
    mix_ref, picked_ref, table_ref, gain_ref, own_gain_ref, proj_hbm, up_hbm, down_hbm,
    attn_ref, out_ref,
    up, down, proj, rows, part, sums, full, acc, hidden, tokens,
    terms, core_in, y_out, y_in, ep_out, ep_in,
    load_sem, row_send, row_recv, rs_send, rs_recv, ag_send, ag_recv, y_send, y_recv,
    c_send, c_recv, t_send, t_recv, tc_send, tc_recv, ty_send, ty_recv, te_send, te_recv,
):
    f32, bf16 = jnp.float32, jnp.bfloat16
    seg, ep = greet(seg_count, ep_count)
    y_count = seg_count // 2
    core, y = lax.rem(seg, 2), lax.div(seg, 2)
    mate = seg + 1 - 2 * core
    own_rows, width = picked_ref.shape
    total = own_rows * seg_count
    chunk = total // ep_count
    cols = proj.shape[1]
    rows[seg] = picked_ref[...]
    moved = []
    for k in range(1, seg_count):
        copy = remote(
            picked_ref, rows.at[seg], row_send.at[k], row_recv.at[k],
            seg=lax.rem(seg + k, seg_count),
        )
        copy.start()
        moved.append(copy)
    loads = [
        pltpu.make_async_copy(proj_hbm, proj, load_sem.at[0]),
        pltpu.make_async_copy(up_hbm.at[0], up, load_sem.at[1]),
        pltpu.make_async_copy(down_hbm.at[0], down, load_sem.at[2]),
    ]
    for load in loads:
        load.start()
    for copy in moved:
        copy.wait()
    picked = rows[...].reshape(total, width).astype(f32)
    squares = jnp.sum(picked * picked, axis=1, keepdims=True)
    high = squares.astype(bf16).astype(f32)
    lane = lax.broadcasted_iota(jnp.int32, (total, 128), 1)
    pair = jnp.where(lane < 64, high, squares - high).astype(bf16)
    part[:, :, cols:] = pair.reshape(ep_count, chunk, 128)
    scaled = (picked * own_gain_ref[...]).astype(bf16)
    loads[0].wait()
    for n in range(0, cols, tile):
        part[:, :, n : n + tile] = (
            jnp.dot(scaled, proj[:, n : n + tile], preferred_element_type=f32)
            .astype(bf16)
            .reshape(ep_count, chunk, tile)
        )
    moved = []
    for j in range(1, ep_count):
        other = lax.rem(ep + j, ep_count)
        copy = remote(part.at[other], sums.at[j], rs_send.at[j], rs_recv.at[j], ep=other)
        copy.start()
        moved.append(copy)
    summed = part[ep].astype(f32)
    for j, copy in enumerate(moved):
        copy.wait()
        summed = summed + sums[j + 1].astype(f32)
    features = width * ep_count
    square = summed[:, cols : cols + 1] + summed[:, cols + 64 : cols + 65]
    inv_rms = lax.rsqrt(square / features + epsilon)
    full[seg, ep] = (summed[:, :cols] * inv_rms).astype(bf16)
    gathers = []
    for j in range(1, ep_count):
        other = lax.rem(ep + j, ep_count)
        copy = remote(full.at[seg, ep], full.at[seg, ep], ag_send.at[j], ag_recv.at[j], ep=other)
        copy.start()
        gathers.append(copy)
    y_copies, core_copies = [], []
    for j in range(ep_count):
        if j > 0:
            gathers[j - 1].wait_recv()
        place = full.at[seg, lax.rem(ep - j + ep_count, ep_count)]
        for k in range(1, y_count):
            copy = remote(
                place, place, y_send.at[j, k], y_recv.at[j, k],
                seg=lax.rem(y + k, y_count) * 2 + core,
            )
            copy.start()
            y_copies.append((j, k, copy))
        copy = remote(place, place, c_send.at[j, 0], c_recv.at[j, 0], seg=mate)
        copy.start()
        core_copies.append(copy)
    loads[1].wait()
    acc[...] = jnp.zeros_like(acc)

    def multiply(s):
        def step(n, carry):
            at = pl.multiple_of(n * tile, tile)
            block = full[s, :, :, pl.ds(at, tile)].reshape(total, tile)
            lines = pl.ds(pl.multiple_of(s * cols + n * tile, tile), tile)
            acc[...] += jnp.dot(block, up[lines, :], preferred_element_type=f32)
            return carry

        lax.fori_loop(0, cols // tile, step, 0)

    multiply(seg)
    for j, k, copy in y_copies:
        copy.wait_recv()
        source = lax.rem(y - k + y_count, y_count) * 2 + core
        place = full.at[source, lax.rem(ep - j + ep_count, ep_count)]
        copy = remote(place, place, c_send.at[j, k], c_recv.at[j, k], seg=mate)
        copy.start()
        core_copies.append(copy)
    for k in range(1, y_count):
        multiply(lax.rem(y - k + y_count, y_count) * 2 + core)
    for copy in core_copies:
        copy.wait()
    for copy in gathers:
        copy.wait_send()
    for _, _, copy in y_copies:
        copy.wait_send()
    backs = []
    tokens[ep] = mix_ref[ep]
    for j in range(1, ep_count):
        other = lax.rem(ep + j, ep_count)
        copy = remote(mix_ref.at[other], tokens.at[ep], t_send.at[j], t_recv.at[j], ep=other)
        copy.start()
        backs.append(copy)
    for k in range(y_count):
        multiply(lax.rem(y + k, y_count) * 2 + 1 - core)
    value = acc[...]
    hidden[...] = (value / (1.0 + jnp.exp(-value))).astype(bf16)
    table = table_ref[...].reshape(total, 128)
    gate = jnp.sum(jnp.where(lane == lax.div(ep, 2), table, 0.0), axis=1, keepdims=True)
    loads[2].wait()
    steps = seg_count
    core_moves, y_moves, ep_moves = {}, {}, {}

    def product(c):
        for n in range(0, cols, tile):
            at = c * cols + n
            value = jnp.dot(hidden[...], down[:, at : at + tile], preferred_element_type=f32)
            value = jnp.where(gate != 0.0, value * gate, 0.0).astype(bf16)
            terms[c, :, :, n : n + tile] = value.reshape(seg_count, own_rows, tile)
        core_moves[c] = []
        for k in range(y_count):
            copy = remote(
                terms.at[c, k * 2 + 1 - core], core_in.at[c, k],
                tc_send.at[c, k], tc_recv.at[c, k], seg=mate,
            )
            copy.start()
            core_moves[c].append(copy)

    def across(c):
        for copy in core_moves[c]:
            copy.wait()
        y_moves[c] = []
        for k in range(1, y_count):
            other = lax.rem(y + k, y_count)
            y_out[c, k] = (
                terms[c, other * 2 + core].astype(f32) + core_in[c, other].astype(f32)
            ).astype(bf16)
            copy = remote(
                y_out.at[c, k], y_in.at[c, k], ty_send.at[c, k], ty_recv.at[c, k],
                seg=other * 2 + core,
            )
            copy.start()
            y_moves[c].append(copy)

    def along(c):
        value = terms[c, seg].astype(f32) + core_in[c, y].astype(f32)
        for k, copy in enumerate(y_moves[c]):
            copy.wait()
            value = value + y_in[c, k + 1].astype(f32)
        ep_out[c] = value.astype(bf16).reshape(ep_count, own_rows // ep_count, cols)
        ep_moves[c] = []
        for j in range(1, ep_count):
            other = lax.rem(ep + j, ep_count)
            copy = remote(
                ep_out.at[c, other], ep_in.at[c, j], te_send.at[c, j], te_recv.at[c, j], ep=other
            )
            copy.start()
            ep_moves[c].append(copy)

    for c in range(steps + 2):
        if c < steps:
            product(c)
        if 0 <= c - 1 < steps:
            across(c - 1)
        if 0 <= c - 2 < steps:
            along(c - 2)
    for copy in backs:
        copy.wait()
    mixed = [tokens[p].astype(f32) for p in range(ep_count)]
    square = sum(jnp.sum(m * m, axis=1, keepdims=True) for m in mixed)
    inv_rms = lax.rsqrt(square / features + epsilon)
    for p in range(ep_count):
        at = slice(p * width, (p + 1) * width)
        attn_ref[:, at] = (mixed[p] * inv_rms * gain_ref[:, at]).astype(bf16)
    for c in range(steps):
        value = ep_out[c, ep].astype(f32)
        for j, copy in enumerate(ep_moves[c]):
            copy.wait()
            value = value + ep_in[c, j + 1].astype(f32)
        out_ref[:, c * cols : (c + 1) * cols] = value.astype(bf16)


def on_device_dense(
    queries, keys, values, log_decay, out_gain, out_proj, experts, gates, up_weight, down_weight
):
    f32, bf16 = jnp.float32, jnp.bfloat16
    dma = pltpu.SemaphoreType.DMA
    seg_count, ep_count = lax.axis_size("seg"), lax.axis_size("ep")
    y_count = seg_count // 2
    tokens_own, features = queries.shape
    length, heads = log_decay.shape
    width = features // ep_count
    dim = width // heads
    moe_own = experts.shape[0]
    seg_rows = moe_own * ep_count
    total = seg_rows * seg_count
    cols = out_proj.shape[1]
    model = up_weight.shape[1]
    units = up_weight.shape[2]
    cumulative = jnp.cumsum(log_decay, axis=0)
    ids = jnp.arange(128, dtype=jnp.int32)[None, None, :]
    table = jnp.sum(jnp.where(experts[:, :, None] == ids, gates[:, :, None], 0.0), axis=1)
    vmem = pl.BlockSpec(memory_space=pltpu.VMEM)
    hbm = pl.BlockSpec(memory_space=pl.ANY)
    mixture, picked, all_gates = pl.pallas_call(
        functools.partial(mix_kernel, seg_count, ep_count, heads, dim),
        out_shape=(
            jax.ShapeDtypeStruct((ep_count, tokens_own, width), bf16),
            jax.ShapeDtypeStruct((seg_rows, width), bf16),
            jax.ShapeDtypeStruct((seg_count, ep_count, moe_own, 128), f32),
        ),
        in_specs=[vmem] * 6,
        out_specs=(vmem,) * 3,
        scratch_shapes=[VM((ep_count, tokens_own, width), bf16)] * 3
        + [VM((seg_count, heads, dim, dim), bf16), VM((seg_count, 8, dim), f32)]
        + [dma((3, ep_count))] * 2
        + [dma((ep_count,))] * 2
        + [dma((seg_count,))] * 6,
        compiler_params=pltpu.CompilerParams(
            collective_id=1, has_side_effects=True, vmem_limit_bytes=48 * 2**20
        ),
    )(queries, keys, values, cumulative, cumulative.T, table)
    own_gain = lax.dynamic_slice_in_dim(out_gain, lax.axis_index("ep") * width, width, 0)
    chunk = total // ep_count
    return pl.pallas_call(
        functools.partial(expert_kernel, seg_count, ep_count, math.gcd(cols, 512)),
        out_shape=(
            jax.ShapeDtypeStruct((tokens_own, features), bf16),
            jax.ShapeDtypeStruct((moe_own, model), bf16),
        ),
        in_specs=[vmem] * 5 + [hbm] * 3,
        out_specs=(vmem, vmem),
        scratch_shapes=[
            VM((model, units), bf16),
            VM((units, model), bf16),
            VM((width, cols), bf16),
            VM((seg_count, seg_rows, width), bf16),
            VM((ep_count, chunk, cols + 128), bf16),
            VM((ep_count, chunk, cols + 128), bf16),
            VM((seg_count, ep_count, chunk, cols), bf16),
            VM((total, units), f32),
            VM((total, units), bf16),
            VM((ep_count, tokens_own, width), bf16),
            VM((seg_count, seg_count, seg_rows, cols), bf16),
            VM((seg_count, y_count, seg_rows, cols), bf16),
            VM((seg_count, y_count, seg_rows, cols), bf16),
            VM((seg_count, y_count, seg_rows, cols), bf16),
            VM((seg_count, ep_count, moe_own, cols), bf16),
            VM((seg_count, ep_count, moe_own, cols), bf16),
            dma((3,)),
        ]
        + [dma((seg_count,))] * 2
        + [dma((ep_count,))] * 4
        + [dma((ep_count, y_count))] * 4
        + [dma((ep_count,))] * 2
        + [dma((seg_count, y_count))] * 4
        + [dma((seg_count, ep_count))] * 2,
        compiler_params=pltpu.CompilerParams(
            collective_id=2, has_side_effects=True, vmem_limit_bytes=60 * 2**20
        ),
    )(mixture, picked, all_gates, out_gain[None, :], own_gain[None, :], out_proj, up_weight, down_weight)


def on_device(*args):
    experts, ep_count = args[6], lax.axis_size("ep")
    full_rows = max(2, 4 * experts.shape[0] // (ep_count // 2)) >= experts.shape[0]
    return (on_device_dense if full_rows else on_device_routed)(*args)


def solution(mesh):
    placed = (
        P(("seg", "ep"), None),
        P(("seg", "ep"), None),
        P(("seg", "ep"), None),
        P("seg", "ep"),
        P(),
        P("ep", "seg"),
        P(("seg", "ep"), None),
        P(("seg", "ep"), None),
        P("ep", None, "seg"),
        P("ep", "seg", None),
    )
    return jax.shard_map(
        on_device,
        mesh=mesh,
        in_specs=placed,
        out_specs=(P(("seg", "ep"), None), P(("seg", "ep"), None)),
        check_vma=False,
    )
```

```python
import functools
import math

import jax
import jax.numpy as jnp
from jax import lax
from jax.experimental import pallas as pl
from jax.experimental.pallas import tpu as pltpu
from jax.sharding import PartitionSpec as P

epsilon = 1e-06
MESH = pl.DeviceIdType.MESH
VM = pltpu.VMEM


def prefix(x, axis, join, neutral):
    place = lax.axis_index(axis)
    gathered = jax.tree.map(
        lambda a, kind: lax.all_gather(a.astype(kind), axis), x, (jnp.bfloat16, jnp.bfloat16)
    )
    state = jax.tree.map(lambda a, e: jnp.zeros_like(a) + jnp.asarray(e, a.dtype), x, neutral)

    def one(turn, state):
        return join(
            state,
            jax.tree.map(
                lambda a, own: lax.dynamic_index_in_dim(a, turn, 0, False).astype(own.dtype),
                gathered,
                x,
            ),
        )

    return lax.fori_loop(0, place, one, state)


def chain_combine(first_part, second_part):
    return (
        first_part[0] * second_part[0],
        second_part[0][:, None, None] * first_part[1] + second_part[1],
    )


def route_tables(experts, gates, expert_count, capacity):
    token_count = experts.shape[0]
    flattened = experts.reshape(-1)
    onehot = (flattened[:, None] == jnp.arange(expert_count, dtype=jnp.int32)[None, :]).astype(
        jnp.int32
    )
    earlier = jnp.cumsum(onehot, axis=0) - onehot
    position = jnp.sum(earlier * onehot, axis=1)
    slot_index = (flattened * capacity + position).reshape(token_count, 2)
    columns = jnp.arange(expert_count * capacity, dtype=jnp.int32)
    matches = slot_index[:, :, None] == columns[None, None, :]
    dispatch = jnp.any(matches, axis=1).T.astype(jnp.bfloat16)
    combine = jnp.sum(jnp.where(matches, gates[:, :, None], 0.0), axis=1)
    return (dispatch, combine)


def expert_output(row_data, up_piece, down_piece):
    hidden = jax.nn.silu(jnp.dot(row_data, up_piece, preferred_element_type=jnp.float32)).astype(
        jnp.bfloat16
    )
    return jnp.dot(hidden, down_piece, preferred_element_type=jnp.float32)


def on_device_routed(
    queries, keys, values, log_decay, out_gain, out_proj, experts, gates, up_weight, down_weight
):
    highest = lax.Precision.HIGHEST
    ep_count = lax.axis_size("ep")
    heads_local = log_decay.shape[1]
    head_dim = queries.shape[1] // (heads_local * ep_count)
    query_heads, key_heads, value_heads = (
        lax.all_to_all(queries, "ep", split_axis=1, concat_axis=0, tiled=True),
        lax.all_to_all(keys, "ep", split_axis=1, concat_axis=0, tiled=True),
        lax.all_to_all(values, "ep", split_axis=1, concat_axis=0, tiled=True),
    )
    seg_length = query_heads.shape[0]
    query_heads = query_heads.reshape(seg_length, heads_local, head_dim)
    key_heads = key_heads.reshape(seg_length, heads_local, head_dim)
    value_heads = value_heads.reshape(seg_length, heads_local, head_dim)
    cumulative = jnp.cumsum(log_decay, axis=0)
    across = cumulative.T
    block_size = math.gcd(seg_length, 512)
    starts = jnp.arange(seg_length // block_size, dtype=jnp.int32) * block_size
    token_positions = jnp.arange(seg_length, dtype=jnp.int32)

    def block_mix(start):
        query_block = lax.dynamic_slice_in_dim(query_heads, start, block_size, 0)
        cum_block = lax.dynamic_slice_in_dim(across, start, block_size, 1)
        row_ids = start + jnp.arange(block_size, dtype=jnp.int32)
        causal = (row_ids[:, None] >= token_positions[None, :])[None]
        log_gap = cum_block[:, :, None] - across[:, None, :]
        weight = jnp.where(causal, jnp.exp(jnp.where(causal, log_gap, 0.0)), 0.0)
        scores = jnp.einsum(
            "thd,shd->hts", query_block, key_heads, preferred_element_type=jnp.float32
        )
        mixing = (scores * weight).astype(jnp.bfloat16)
        return jnp.einsum("hts,she->the", mixing, value_heads, preferred_element_type=jnp.float32)

    inside = lax.map(block_mix, starts).reshape(seg_length, heads_local, head_dim)
    ending = cumulative[-1]
    to_end = jnp.exp(ending[None, :] - cumulative)
    key_float = key_heads.astype(jnp.float32)
    value_float = value_heads.astype(jnp.float32)
    local_state = jnp.einsum("sh,shd,she->hde", to_end, key_float, value_float, precision=highest)
    identity = (jnp.ones_like(ending), jnp.zeros_like(local_state))
    carried = prefix((jnp.exp(ending), local_state), "seg", chain_combine, identity)[1]
    outside = jnp.exp(cumulative)[:, :, None] * jnp.einsum(
        "thd,hde->the", query_heads.astype(jnp.float32), carried, precision=highest
    )
    mixture = (inside + outside).astype(jnp.bfloat16).reshape(seg_length, heads_local * head_dim)
    token_mix = lax.all_to_all(mixture, "ep", split_axis=0, concat_axis=1, tiled=True)
    as_float = token_mix.astype(jnp.float32)
    inv_rms = lax.rsqrt(jnp.mean(as_float * as_float, axis=1, keepdims=True) + epsilon)
    attn_out = (as_float * inv_rms * out_gain[None, :]).astype(jnp.bfloat16)
    row_stride = 8
    own_width = heads_local * head_dim
    feature_count = own_width * ep_count
    picked_float = mixture.reshape(seg_length // row_stride, row_stride, own_width)[:, 0].astype(
        jnp.float32
    )
    square_sums = lax.psum(jnp.sum(picked_float * picked_float, axis=1), "ep")
    picked_rms = lax.rsqrt(square_sums[:, None] / feature_count + epsilon)
    gain_slice = lax.dynamic_slice_in_dim(out_gain, lax.axis_index("ep") * own_width, own_width, 0)
    normed_rows = (picked_float * picked_rms * gain_slice[None, :]).astype(jnp.bfloat16)
    proj_terms = jnp.dot(
        normed_rows,
        lax.all_gather(out_proj, "seg", axis=1, tiled=True),
        preferred_element_type=jnp.float32,
    )
    moe_in = lax.psum_scatter(
        proj_terms.astype(jnp.bfloat16), "ep", scatter_dimension=0, tiled=True
    )
    expert_count = ep_count // 2
    token_count, model_width = moe_in.shape
    capacity = max(2, 4 * token_count // expert_count)
    dispatch, combine = route_tables(experts, gates, expert_count, capacity)
    up_piece = up_weight[0]
    down_piece = down_weight[0]
    slot_rows = jnp.dot(dispatch, moe_in, preferred_element_type=jnp.float32).astype(jnp.bfloat16)
    outgoing = jnp.repeat(slot_rows.reshape(expert_count, capacity, model_width), 2, axis=0)
    arrived = lax.all_to_all(outgoing, "ep", split_axis=0, concat_axis=0, tiled=True).reshape(
        ep_count * capacity, model_width
    )
    gathered = lax.all_gather(arrived, "seg", axis=0, tiled=True)
    owned_sums = lax.psum_scatter(
        expert_output(gathered, up_piece, down_piece).astype(jnp.bfloat16),
        "seg",
        scatter_dimension=0,
        tiled=True,
    ).astype(jnp.float32)
    returned_back = lax.all_to_all(
        owned_sums.reshape(ep_count, capacity, model_width).astype(jnp.bfloat16),
        "ep",
        split_axis=0,
        concat_axis=0,
        tiled=True,
    ).astype(jnp.float32)
    paired = returned_back.reshape(expert_count, 2, capacity, model_width)
    halves = (paired[:, 0] + paired[:, 1]).reshape(expert_count * capacity, model_width)
    summed = jnp.dot(combine, halves, precision=highest)
    moe_out = summed.astype(jnp.bfloat16)
    return (attn_out, moe_out)


def remote(src, dst, send, recv, **target):
    return pltpu.make_async_remote_copy(
        src_ref=src, dst_ref=dst, send_sem=send, recv_sem=recv,
        device_id=target, device_id_type=MESH,
    )


def greet(seg_count, ep_count):
    seg, ep = lax.axis_index("seg"), lax.axis_index("ep")
    barrier = pltpu.get_barrier_semaphore()
    for j in range(1, ep_count):
        pl.semaphore_signal(
            barrier, inc=1, device_id={"ep": lax.rem(ep + j, ep_count)}, device_id_type=MESH
        )
    for k in range(1, seg_count):
        pl.semaphore_signal(
            barrier, inc=1, device_id={"seg": lax.rem(seg + k, seg_count)}, device_id_type=MESH
        )
    pl.semaphore_wait(barrier, ep_count + seg_count - 2)
    return seg, ep


def step_kernel(
    seg_count, ep_count, heads, dim, tile,
    q_ref, k_ref, v_ref, proj_hbm, up_hbm, down_hbm,
    decay_ref, turned_ref, experts_ref, gates_ref, gain_ref,
    attn_ref, out_ref,
    qb, kb, vb, states, ends, table_ref, mix_ref,
    up, down, proj, rows, part, sums, full, acc, hidden, tokens,
    terms, core_in, both, y_in, x_in, middle, line, line_in,
    load_sem, in_send, in_recv, gate_send, gate_recv,
    st_send, st_recv, end_send, end_recv, row_send, row_recv, pick_send, pick_recv,
    rs_send, rs_recv, ag_send, ag_recv, x_send, x_recv, y_send, y_recv, c_send, c_recv,
    t_send, t_recv, tc_send, tc_recv, ty_send, ty_recv, tx_send, tx_recv, tz_send, tz_recv,
):
    seg, ep = greet(seg_count, ep_count)
    width = heads * dim
    tokens_own, moe_own = q_ref.shape[0], experts_ref.shape[0]
    triples = ((k_ref, kb), (v_ref, vb), (q_ref, qb))
    sends = {}
    own = pl.ds(pl.multiple_of(ep * width, width), width)
    keep = []
    for i, (ref, buf) in enumerate(triples):
        sends[i] = []
        for j in range(1, ep_count):
            other = lax.rem(ep + j, ep_count)
            columns = pl.ds(pl.multiple_of(other * width, width), width)
            copy = remote(
                ref.at[:, columns], buf.at[ep], in_send.at[i, j], in_recv.at[i, j], ep=other
            )
            copy.start()
            sends[i].append(copy)
        copy = pltpu.make_async_copy(ref.at[:, own], buf.at[ep], load_sem.at[3 + i])
        copy.start()
        keep.append(copy)
    loads = [
        pltpu.make_async_copy(proj_hbm, proj, load_sem.at[0]),
        pltpu.make_async_copy(up_hbm.at[0], up, load_sem.at[1]),
        pltpu.make_async_copy(down_hbm.at[0], down, load_sem.at[2]),
    ]
    for load in loads:
        load.start()
    lanes = lax.broadcasted_iota(jnp.int32, (moe_own, 128), 1)
    table_ref[seg, ep] = sum(
        jnp.where(experts_ref[:, i : i + 1] == lanes, gates_ref[:, i : i + 1], 0.0)
        for i in range(experts_ref.shape[1])
    )
    gates = []
    for j in range(1, ep_count):
        copy = remote(
            table_ref.at[seg, ep], table_ref.at[seg, ep], gate_send.at[j], gate_recv.at[j],
            ep=lax.rem(ep + j, ep_count),
        )
        copy.start()
        gates.append(copy)
    length = tokens_own * ep_count
    highest = lax.Precision.HIGHEST
    rows_at = lax.broadcasted_iota(jnp.int32, (length, length), 0)
    columns_at = lax.broadcasted_iota(jnp.int32, (length, length), 1)
    causal = rows_at >= columns_at
    lower = causal.astype(jnp.float32)
    cum = jnp.dot(lower, decay_ref[...], precision=highest, preferred_element_type=jnp.float32)
    across = lax.dot_general(
        turned_ref[...], lower, (((1,), (1,)), ((), ())), precision=highest,
        preferred_element_type=jnp.float32,
    )
    for copy in keep:
        copy.wait()
    for i in (0, 1):
        for copy in sends[i]:
            copy.wait()
    keys, values = (
        jnp.concatenate([b[p] for p in range(ep_count)], axis=0) for b in (kb, vb)
    )
    ending = cum[length - 1 : length, :]
    unit = (
        lax.broadcasted_iota(jnp.int32, (dim, dim), 0)
        == lax.broadcasted_iota(jnp.int32, (dim, dim), 1)
    ).astype(jnp.float32).astype(jnp.bfloat16)
    for h in range(heads):
        cols = slice(h * dim, (h + 1) * dim)
        to_end = jnp.exp(ending[:, h : h + 1] - across[h : h + 1, :])
        turned = lax.dot_general(
            unit, keys[:, cols], (((1,), (1,)), ((), ())), preferred_element_type=jnp.float32
        )
        states[seg, h] = jnp.dot(
            (turned * to_end).astype(jnp.bfloat16), values[:, cols],
            preferred_element_type=jnp.float32,
        ).astype(jnp.bfloat16)
        ends[seg, h : h + 1] = jnp.broadcast_to(ending[:, h : h + 1], (1, dim))
    for copy in gates:
        copy.wait()
    moved = []
    for k in range(1, seg_count):
        other = lax.rem(seg + k, seg_count)
        for buf, send, recv in (
            (states, st_send, st_recv), (ends, end_send, end_recv), (table_ref, row_send, row_recv)
        ):
            copy = remote(buf.at[seg], buf.at[seg], send.at[k], recv.at[k], seg=other)
            copy.start()
            moved.append(copy)
    for copy in sends[2]:
        copy.wait()
    queries = jnp.concatenate([qb[p] for p in range(ep_count)], axis=0)
    inside = []
    for h in range(heads):
        cols = slice(h * dim, (h + 1) * dim)
        gap = cum[:, h : h + 1] - across[h : h + 1, :]
        weight = jnp.where(causal, jnp.exp(jnp.where(causal, gap, 0.0)), 0.0)
        scores = lax.dot_general(
            queries[:, cols], keys[:, cols], (((1,), (1,)), ((), ())),
            preferred_element_type=jnp.float32,
        )
        inside.append(
            jnp.dot(
                (scores * weight).astype(jnp.bfloat16), values[:, cols],
                preferred_element_type=jnp.float32,
            )
        )
    for copy in moved:
        copy.wait()
    outs = []
    for h in range(heads):
        cols = slice(h * dim, (h + 1) * dim)
        carried = jnp.zeros((dim, dim), jnp.float32)
        for c in range(seg_count):
            joined = jnp.exp(ends[c, h : h + 1]) * carried + states[c, h].astype(jnp.float32)
            carried = jnp.where(c < seg, joined, carried)
        outside = jnp.exp(cum[:, h : h + 1]) * jnp.dot(
            queries[:, cols], carried.astype(jnp.bfloat16), preferred_element_type=jnp.float32
        )
        outs.append((inside[h] + outside).astype(jnp.bfloat16))
    mixture = jnp.concatenate(outs, axis=1)
    mix_ref[...] = mixture.reshape(mix_ref.shape)
    count = length // tokens_own * moe_own
    stride = length // count
    pick = (
        lax.broadcasted_iota(jnp.int32, (count, length), 1)
        == stride * lax.broadcasted_iota(jnp.int32, (count, length), 0)
    )
    rows[seg] = jnp.dot(
        pick.astype(jnp.float32).astype(jnp.bfloat16), mixture, preferred_element_type=jnp.float32
    ).astype(jnp.bfloat16)
    f32, bf16 = jnp.float32, jnp.bfloat16
    y_count = seg_count // 2
    core, y = lax.rem(seg, 2), lax.div(seg, 2)
    mate = seg + 1 - 2 * core
    own_rows = rows.shape[1]
    total = own_rows * seg_count
    chunk = total // ep_count
    cols = proj.shape[1]
    moved = []
    for k in range(1, seg_count):
        copy = remote(
            rows.at[seg], rows.at[seg], pick_send.at[k], pick_recv.at[k],
            seg=lax.rem(seg + k, seg_count),
        )
        copy.start()
        moved.append(copy)
    for copy in moved:
        copy.wait()
    picked = rows[...].reshape(total, width).astype(f32)
    squares = jnp.sum(picked * picked, axis=1, keepdims=True)
    high = squares.astype(bf16).astype(f32)
    lane = lax.broadcasted_iota(jnp.int32, (total, 128), 1)
    pair = jnp.where(lane < 64, high, squares - high).astype(bf16)
    part[:, :, cols:] = pair.reshape(ep_count, chunk, 128)
    scaled = (picked * gain_ref[:, own]).astype(bf16)
    loads[0].wait()
    for n in range(0, cols, tile):
        part[:, :, n : n + tile] = (
            jnp.dot(scaled, proj[:, n : n + tile], preferred_element_type=f32)
            .astype(bf16)
            .reshape(ep_count, chunk, tile)
        )
    moved = []
    for j in range(1, ep_count):
        other = lax.rem(ep + j, ep_count)
        copy = remote(part.at[other], sums.at[j], rs_send.at[j], rs_recv.at[j], ep=other)
        copy.start()
        moved.append(copy)
    summed = part[ep].astype(f32)
    for j, copy in enumerate(moved):
        copy.wait()
        summed = summed + sums[j + 1].astype(f32)
    features = width * ep_count
    square = summed[:, cols : cols + 1] + summed[:, cols + 64 : cols + 65]
    inv_rms = lax.rsqrt(square / features + epsilon)
    full[seg, ep] = (summed[:, :cols] * inv_rms).astype(bf16)
    half = ep_count // 2
    x, z = lax.rem(ep, 2), lax.div(ep, 2)
    x_mate = ep + 1 - 2 * x
    flying = []

    def send(place, send_sem, recv_sem, **target):
        copy = remote(place, place, send_sem, recv_sem, **target)
        copy.start()
        flying.append(copy)
        return copy

    def on_line(e, k):
        return lax.rem(e - 2 * k + ep_count, ep_count)

    def y_seg(k):
        return lax.rem(y + k + y_count, y_count) * 2 + core

    z_copies = {}
    for k in range(1, half):
        z_copies[k] = send(
            full.at[seg, ep], ag_send.at[k], ag_recv.at[k], ep=lax.rem(ep + 2 * k, ep_count)
        )
    x_copies, y_copies = {}, {}
    for k in range(half):
        if k > 0:
            z_copies[k].wait_recv()
        place = full.at[seg, on_line(ep, k)]
        x_copies[k, 0] = send(place, x_send.at[k, 0], x_recv.at[k, 0], ep=x_mate)
        for d in range(1, y_count):
            y_copies[k, 0, d] = send(
                place, y_send.at[k, 0, d], y_recv.at[k, 0, d], seg=y_seg(d)
            )
        send(place, c_send.at[k, 0, 0], c_recv.at[k, 0, 0], seg=mate)
    for k in range(half):
        x_copies[k, 0].wait_recv()
        place = full.at[seg, on_line(x_mate, k)]
        if k % 2 == 0:
            for d in range(1, y_count):
                y_copies[k, 1, d] = send(
                    place, y_send.at[k, 1, d], y_recv.at[k, 1, d], seg=y_seg(d)
                )
        send(place, c_send.at[k, 1, 0], c_recv.at[k, 1, 0], seg=mate)
        for d in range(1, y_count):
            y_copies[k, 0, d].wait_recv()
            place = full.at[y_seg(-d), on_line(ep, k)]
            if k % 2 == 1:
                x_copies[k, d] = send(place, x_send.at[k, d], x_recv.at[k, d], ep=x_mate)
            send(place, c_send.at[k, 0, d], c_recv.at[k, 0, d], seg=mate)
    loads[1].wait()
    acc[...] = jnp.zeros_like(acc)

    def multiply(s):
        def step(n, carry):
            at = pl.multiple_of(n * tile, tile)
            block = full[s, :, :, pl.ds(at, tile)].reshape(total, tile)
            lines = pl.ds(pl.multiple_of(s * cols + n * tile, tile), tile)
            acc[...] += lax.dot_general(
                block, up[:, lines], (((1,), (1,)), ((), ())), preferred_element_type=f32
            )
            return carry

        lax.fori_loop(0, cols // tile, step, 0)

    multiply(seg)
    for k in range(half):
        for d in range(1, y_count):
            (y_copies[k, 1, d] if k % 2 == 0 else x_copies[k, d]).wait_recv()
            send(
                full.at[y_seg(-d), on_line(x_mate, k)],
                c_send.at[k, 1, d], c_recv.at[k, 1, d], seg=mate,
            )
    for d in range(1, y_count):
        multiply(y_seg(-d))
    for k in range(half):
        for i in range(2):
            for d in range(y_count):
                place = full.at[seg, ep]
                remote(place, place, c_send.at[k, i, d], c_recv.at[k, i, d], seg=mate).wait_recv()
    for copy in flying:
        copy.wait_send()
    backs = []
    tokens[ep] = mix_ref[ep]
    for j in range(1, ep_count):
        other = lax.rem(ep + j, ep_count)
        copy = remote(mix_ref.at[other], tokens.at[ep], t_send.at[j], t_recv.at[j], ep=other)
        copy.start()
        backs.append(copy)
    for k in range(y_count):
        multiply(lax.rem(y + k, y_count) * 2 + 1 - core)
    value = acc[...]
    hidden[...] = (value / (1.0 + jnp.exp(-value))).astype(bf16)
    table = table_ref[...].reshape(total, 128)
    gate = jnp.sum(jnp.where(lane == lax.div(ep, 2), table, 0.0), axis=1, keepdims=True)
    loads[2].wait()
    steps = seg_count
    core_moves = {}

    def product(c):
        for n in range(0, cols, tile):
            at = c * cols + n
            value = jnp.dot(hidden[...], down[:, at : at + tile], preferred_element_type=f32)
            value = jnp.where(gate != 0.0, value * gate, 0.0).astype(bf16)
            terms[c, :, :, n : n + tile] = value.reshape(seg_count, own_rows, tile)
        core_moves[c] = []
        for k in range(y_count):
            copy = remote(
                terms.at[c, k * 2 + 1 - core], core_in.at[c, k],
                tc_send.at[c, k], tc_recv.at[c, k], seg=mate,
            )
            copy.start()
            core_moves[c].append(copy)

    first, second, last = {}, {}, {}
    mine = own_rows // ep_count

    def joined(c):
        for copy in core_moves[c]:
            copy.wait()
        for k in range(y_count):
            value = (terms[c, k * 2 + core].astype(f32) + core_in[c, k].astype(f32)).reshape(
                half, 2, mine, cols
            ).astype(bf16)
            for i in range(2):
                both[c, k, i] = value[:, i]
        first[c] = []
        if c % 2 == 0:
            for d in range(1, y_count):
                first[c].append(
                    remote(
                        both.at[c, lax.rem(y + d, y_count)], y_in.at[c, d],
                        ty_send.at[c, d], ty_recv.at[c, d], seg=y_seg(d),
                    )
                )
        else:
            first[c].append(
                remote(
                    both.at[c, :, 1 - x], x_in.at[c], tx_send.at[c], tx_recv.at[c], ep=x_mate
                )
            )
        for copy in first[c]:
            copy.start()

    def crossed(c):
        for copy in first[c]:
            copy.wait()
        second[c] = []
        if c % 2 == 0:
            for i in range(2):
                value = both[c, y, i].astype(f32)
                for d in range(1, y_count):
                    value = value + y_in[c, d, i].astype(f32)
                middle[c, i] = value.astype(bf16)
            second[c].append(
                remote(
                    middle.at[c, 1 - x], x_in.at[c, 0], tx_send.at[c], tx_recv.at[c], ep=x_mate
                )
            )
        else:
            for k in range(y_count):
                middle[c, k] = (both[c, k, x].astype(f32) + x_in[c, k].astype(f32)).astype(bf16)
            for d in range(1, y_count):
                second[c].append(
                    remote(
                        middle.at[c, lax.rem(y + d, y_count)], y_in.at[c, d, 0],
                        ty_send.at[c, d], ty_recv.at[c, d], seg=y_seg(d),
                    )
                )
        for copy in second[c]:
            copy.start()

    def along(c):
        for copy in second[c]:
            copy.wait()
        if c % 2 == 0:
            value = middle[c, x].astype(f32) + x_in[c, 0].astype(f32)
        else:
            value = middle[c, y].astype(f32)
            for d in range(1, y_count):
                value = value + y_in[c, d, 0].astype(f32)
        line[c] = value.astype(bf16)
        last[c] = []
        for k in range(1, half):
            other = lax.rem(z + k, half)
            copy = remote(
                line.at[c, other], line_in.at[c, k], tz_send.at[c, k], tz_recv.at[c, k],
                ep=other * 2 + x,
            )
            copy.start()
            last[c].append(copy)

    for c in range(steps + 3):
        if c < steps:
            product(c)
        if 0 <= c - 1 < steps:
            joined(c - 1)
        if 0 <= c - 2 < steps:
            crossed(c - 2)
        if 0 <= c - 3 < steps:
            along(c - 3)
    for copy in backs:
        copy.wait()
    mixed = [tokens[p].astype(f32) for p in range(ep_count)]
    square = sum(jnp.sum(m * m, axis=1, keepdims=True) for m in mixed)
    inv_rms = lax.rsqrt(square / features + epsilon)
    for p in range(ep_count):
        at = slice(p * width, (p + 1) * width)
        attn_ref[:, at] = (mixed[p] * inv_rms * gain_ref[:, at]).astype(bf16)
    for c in range(steps):
        value = line[c, z].astype(f32)
        for j, copy in enumerate(last[c]):
            copy.wait()
            value = value + line_in[c, j + 1].astype(f32)
        out_ref[:, c * cols : (c + 1) * cols] = value.astype(bf16)


def on_device_dense(
    queries, keys, values, log_decay, out_gain, out_proj, experts, gates, up_weight, down_weight
):
    f32, bf16 = jnp.float32, jnp.bfloat16
    dma = pltpu.SemaphoreType.DMA
    seg_count, ep_count = lax.axis_size("seg"), lax.axis_size("ep")
    y_count, half = seg_count // 2, ep_count // 2
    tokens_own, features = queries.shape
    heads = log_decay.shape[1]
    width = features // ep_count
    dim = width // heads
    moe_own = experts.shape[0]
    seg_rows = moe_own * ep_count
    total = seg_rows * seg_count
    cols = out_proj.shape[1]
    model, units = up_weight.shape[1:]
    chunk = total // ep_count
    vmem = pl.BlockSpec(memory_space=pltpu.VMEM)
    hbm = pl.BlockSpec(memory_space=pl.ANY)
    return pl.pallas_call(
        functools.partial(step_kernel, seg_count, ep_count, heads, dim, math.gcd(cols, 512)),
        out_shape=(
            jax.ShapeDtypeStruct((tokens_own, features), bf16),
            jax.ShapeDtypeStruct((moe_own, model), bf16),
        ),
        in_specs=[hbm] * 6 + [vmem] * 5,
        out_specs=(vmem, vmem),
        scratch_shapes=[VM((ep_count, tokens_own, width), bf16)] * 3
        + [
            VM((seg_count, heads, dim, dim), bf16),
            VM((seg_count, 8, dim), f32),
            VM((seg_count, ep_count, moe_own, 128), f32),
            VM((ep_count, tokens_own, width), bf16),
            VM((units, model), bf16),
            VM((units, model), bf16),
            VM((width, cols), bf16),
            VM((seg_count, seg_rows, width), bf16),
            VM((ep_count, chunk, cols + 128), bf16),
            VM((ep_count, chunk, cols + 128), bf16),
            VM((seg_count, ep_count, chunk, cols), bf16),
            VM((total, units), f32),
            VM((total, units), bf16),
            VM((ep_count, tokens_own, width), bf16),
            VM((seg_count, seg_count, seg_rows, cols), bf16),
            VM((seg_count, y_count, seg_rows, cols), bf16),
            VM((seg_count, y_count, 2, half, moe_own, cols), bf16),
            VM((seg_count, y_count, 2, half, moe_own, cols), bf16),
            VM((seg_count, y_count, half, moe_own, cols), bf16),
            VM((seg_count, max(2, y_count), half, moe_own, cols), bf16),
            VM((seg_count, half, moe_own, cols), bf16),
            VM((seg_count, half, moe_own, cols), bf16),
            dma((6,)),
        ]
        + [dma((3, ep_count))] * 2
        + [dma((ep_count,))] * 2
        + [dma((seg_count,))] * 8
        + [dma((ep_count,))] * 2
        + [dma((half,))] * 2
        + [dma((half, y_count))] * 2
        + [dma((half, 2, y_count))] * 4
        + [dma((ep_count,))] * 2
        + [dma((seg_count, y_count))] * 4
        + [dma((seg_count,))] * 2
        + [dma((seg_count, half))] * 2,
        compiler_params=pltpu.CompilerParams(
            collective_id=1, has_side_effects=True, vmem_limit_bytes=62 * 2**20
        ),
    )(
        queries, keys, values, out_proj, jnp.swapaxes(up_weight, 1, 2), down_weight,
        log_decay, log_decay.T, experts, gates, out_gain[None, :],
    )


def on_device(*args):
    experts, ep_count = args[6], lax.axis_size("ep")
    full_rows = max(2, 4 * experts.shape[0] // (ep_count // 2)) >= experts.shape[0]
    return (on_device_dense if full_rows else on_device_routed)(*args)


def solution(mesh):
    placed = (
        P(("seg", "ep"), None),
        P(("seg", "ep"), None),
        P(("seg", "ep"), None),
        P("seg", "ep"),
        P(),
        P("ep", "seg"),
        P(("seg", "ep"), None),
        P(("seg", "ep"), None),
        P("ep", None, "seg"),
        P("ep", "seg", None),
    )
    return jax.shard_map(
        on_device,
        mesh=mesh,
        in_specs=placed,
        out_specs=(P(("seg", "ep"), None), P(("seg", "ep"), None)),
        check_vma=False,
    )
```
